512 devices in a mesh: row: 16 (over z, core), col: 32 (over x, y).
Axes of the slice: x: 4, y: 8, z: 8, core: 2. Of those that a mesh axis runs over, the one named last changes fastest.
Arguments:
- u_front: bfloat16 [2, 2048, 25, 2048], P(None, 'col', None, 'row'), may hold values from -0.02734375 to 0.02734375
- inverse_blocks: bfloat16 [2, 2048, 1, 2048], P(None, 'col', None, 'row')
- rhs_window: float32 [32, 2, 2048], P(None, None, 'col'), may hold values from -6 to 6
- pivot_inverse: float32 [2, 2048], P(None, 'col'), may hold values from 0.25 to 4
- below_solution: bfloat16 [32, 23, 2048], P(None, None, 'row'), may hold values from -6 to 6
- u_child: bfloat16 [4096, 16, 2048], P('col', None, 'row'), may hold values from -0.03125 to 0.03125
- rhs_child: float32 [32, 4096], P(None, 'col'), may hold values from -6 to 6
- child_map: int32 [2, 256], replicated, may hold values from 0 to 399, as said below
- child_counts: int32 [2], replicated, may hold values from 128 to 256, as said below
Outputs:
- x_window: float32 [32, 2, 2048], P(None, None, 'row')
- child_out: float32 [32, 4096], P(None, 'col')
The draws below stay inside these ranges and needn't reach their ends.
Inputs may be any that keep to these rules, and one draw needn't show every extreme that they name: Slot s of a child lies on row index s % 16 of the child's rows, and the block it names lies on row index (s % 16 + s // 16) % 16 of the front's rows, that is child_map[h, s] % 16 equals that number; one child names each block at most once; both ends of the range are named. `child_counts`: one of the two children uses all 256 slots.
All inputs are finite; a program needn't handle non-finite values.
Results may differ from the reference program's by a relative error of at most 0.003.
Values may be sent and summed in bfloat16 or wider, within the bound.
A program may use at most 64 MiB of HBM per device.

```python
import math
import jax
import jax.numpy as jnp
from jax import lax

NB = 128
PB = 2048
PANELS = 2
NF = 51200
NRHS = 32
CBLK = 256
RBD = 25
BRB = 23
PRB = 1
SBD = 16
N_ROW = 16


def draw_inverse_blocks(key, part):
    group_rows = PB // PRB
    extent = (PANELS, PB, PRB, group_rows)
    values = jax.random.normal(key, extent, jnp.float32)
    first_index = lax.broadcasted_iota(jnp.int32, extent, 1)
    second_index = lax.broadcasted_iota(jnp.int32, extent, 2) * group_rows + lax.broadcasted_iota(jnp.int32, extent, 3)
    below_mask = (first_index > second_index).astype(jnp.float32)
    diagonal = (first_index == second_index).astype(jnp.float32)
    return (diagonal + below_mask * values * (0.7 / math.sqrt(PB))).astype(jnp.bfloat16)


def force_front(order, wanted_value):
    where_value = jnp.argmax((order == wanted_value).astype(jnp.int32)).astype(jnp.int32)
    first_value = order[0]
    order = order.at[where_value].set(first_value)
    return order.at[0].set(wanted_value)


def draw_child_map(key, part):
    row_count = N_ROW
    blocks_dev = NF // (NB * N_ROW)

    def one_child(child_key):
        source_keys = jax.random.split(child_key, row_count)
        orders = jax.vmap(lambda inner_key: jax.random.permutation(inner_key, blocks_dev))(source_keys).astype(jnp.int32)
        orders = orders.at[0].set(force_front(orders[0], 0))
        orders = orders.at[row_count - 1].set(force_front(orders[row_count - 1], blocks_dev - 1))
        slot_ids = jnp.arange(CBLK, dtype=jnp.int32)
        target = slot_ids % row_count
        within = slot_ids // row_count
        source = (target + within) % row_count
        chosen = orders[source, within].astype(jnp.int32)
        return chosen * row_count + source
    child_keys = jax.random.split(jax.random.fold_in(key, 7), 2)
    return jax.vmap(one_child)(child_keys).astype(jnp.int32)


def draw_child_counts(key, part):
    fuller = jax.random.randint(jax.random.fold_in(key, 3), (), 0, 2)
    other_count = jax.random.randint(jax.random.fold_in(key, 5), (), CBLK // 2, CBLK + 1)
    first_count = jnp.where(fuller == 0, CBLK, other_count)
    second_count = jnp.where(fuller == 0, other_count, CBLK)
    return jnp.stack([first_count, second_count]).astype(jnp.int32)


def shard_levels(own_key, dims, shards, least, high):
    gain = 1.0
    for position, shards_of in shards:
        steps = jax.random.uniform(jax.random.fold_in(jax.random.fold_in(own_key, 6), position), (shards_of,), jnp.float32, least / len(shards), high / len(shards))
        gain = gain * jnp.repeat(jnp.exp(steps), dims[position] // shards_of).reshape((-1,) + (1,) * (len(dims) - 1 - position))
    return gain


def centred(own_key, shape, width, reach, shards=(), held_as=jnp.bfloat16):
    values = width * jax.random.normal(own_key, shape, jnp.float32)
    if shards:
        values = values * shard_levels(own_key, shape, shards, -0.22, 0.18)
    return jnp.clip(values, -reach, reach).astype(held_as)


def setup_inputs(seed: int = 0) -> dict:
    key_of = jax.random.split(jax.random.key(seed), 10)
    return {
        "u_front": centred(key_of[0], (PANELS, PB, RBD, N_ROW * NB), NF ** -0.5, 0.02734375, ((1, 32), (3, 16))),
        "inverse_blocks": draw_inverse_blocks(jax.random.fold_in(key_of[9], 71), 0),
        "rhs_window": centred(key_of[2], (NRHS, PANELS, PB), 1.0, 6.0, ((2, 32),), jnp.float32),
        "pivot_inverse": jnp.clip(jnp.exp(math.log(4.0) - 2.7725887 * jax.random.uniform(key_of[3], (PANELS, PB), jnp.float32) ** shard_levels(key_of[3], (PANELS, PB), ((1, 32),), -0.2, 0.2)), 0.25, 4.0),
        "below_solution": centred(key_of[4], (NRHS, BRB, N_ROW * NB), 1.0, 6.0, ((2, 16),)),
        "u_child": centred(key_of[5], (2 * PB, SBD, N_ROW * NB), (CBLK * NB) ** -0.5, 0.03125, ((0, 32), (2, 16))),
        "rhs_child": centred(key_of[6], (NRHS, 2 * PB), 1.0, 6.0, ((1, 32),), jnp.float32),
        "child_map": draw_child_map(jax.random.fold_in(key_of[9], 71), 0),
        "child_counts": draw_child_counts(jax.random.fold_in(key_of[9], 71), 0),
    }


def reference(u_front, inverse_blocks, rhs_window, pivot_inverse, below_solution, u_child, rhs_child, child_map, child_counts):
    window = PANELS * PB
    factor = u_front.reshape(window, NF)
    inverses = inverse_blocks.reshape(PANELS, PB, PB)
    scaled = (rhs_window * pivot_inverse[None]).reshape(NRHS, PANELS, PB)
    solved_low = below_solution.reshape(NRHS, NF - window)
    pieces = []
    for panel_index in reversed(range(PANELS)):
        row_start = (panel_index + 1) * PB
        coeffs = factor[panel_index * PB:(panel_index + 1) * PB, row_start:]
        update = jnp.dot(solved_low, coeffs.T, preferred_element_type=jnp.float32)
        reduced = (scaled[:, panel_index] - update).astype(jnp.bfloat16)
        result = jnp.dot(reduced, inverses[panel_index], preferred_element_type=jnp.float32)
        pieces.insert(0, result)
        solved_low = jnp.concatenate([result.astype(jnp.bfloat16), solved_low], axis=1)
    x_window = jnp.concatenate(pieces, axis=1).reshape(NRHS, window // (N_ROW * NB), N_ROW * NB)
    parent = solved_low.reshape(NRHS, NF // NB, NB)
    child_factor = u_child.reshape(2, PB, CBLK * NB)
    slot_ids = jnp.arange(CBLK, dtype=jnp.int32)
    outputs = []
    for which_child in range(2):
        gathered = jnp.take(parent, child_map[which_child], axis=1)
        live_mask = (slot_ids < child_counts[which_child]).astype(gathered.dtype)
        gathered = (gathered * live_mask[None, :, None]).reshape(NRHS, CBLK * NB)
        update = jnp.dot(gathered, child_factor[which_child].T, preferred_element_type=jnp.float32)
        outputs.append(rhs_child[:, which_child * PB:(which_child + 1) * PB] - update)
    child_out = jnp.concatenate(outputs, axis=1)
    return (x_window, child_out)
```

```python
import functools

import jax
import jax.numpy as jnp
from jax import lax
from jax.experimental import pallas as pl
from jax.experimental.pallas import tpu as pltpu
from jax.sharding import PartitionSpec as P

MESH = pl.DeviceIdType.MESH
F32 = jnp.float32
BF16 = jnp.bfloat16
CORES = 2
ZS = 8
XS = 4
YS = 8
ROWS = ZS * CORES
NT = (((1,), (1,)), ((), ()))
NN = (((1,), (0,)), ((), ()))


def dot(a, b, dims):
    return lax.dot_general(a, b, dims, preferred_element_type=F32)


def kernel(
    u_hbm, inv_hbm, rhs_hbm, piv_hbm, below_hbm, uc_hbm, rc_hbm, map_hbm, cnt_hbm,
    x_out, c_out,
    u, inv, rhs, piv, xb, uc, rc, cmap, cnt,
    ucf, ct, cr, wsel, early,
    l10g, m0g, sy_send, sy_recv, x0y,
    p1a, p1r, p1s, p1z,
    x1p, p2, p3s, p3,
    p4a, p4r, p4s, p4z,
    p5s, p5,
    p7a, p7r, p7s, p7z,
    in_sem, send, recv,
):
    row = lax.axis_index("row")
    col = lax.axis_index("col")
    z = row // CORES
    core = lax.rem(row, CORES)
    xx = col // YS
    yy = lax.rem(col, YS)

    def at_row(d):
        return (lax.rem(row + d, ROWS), col)

    def at_z(d):
        return (lax.rem(z + d, ZS) * CORES + core, col)

    def at_x(d):
        return (row, lax.rem(xx + d, XS) * YS + yy)

    def at_y(d):
        return (row, xx * YS + lax.rem(yy + d, YS))

    sibling = (z * CORES + (1 - core), col)
    z_far_first = (4, 3, 5, 2, 6, 1, 7)
    y_far_first = (4, 3, 5, 2, 6, 1, 7)
    x_far_first = (2, 1, 3)

    barrier = pltpu.get_barrier_semaphore()
    for d in z_far_first:
        for other in (0, 1):
            pl.semaphore_signal(
                barrier, inc=1, device_id=(lax.rem(z + d, ZS) * CORES + other, col), device_id_type=MESH
            )
    for d in y_far_first:
        pl.semaphore_signal(barrier, inc=1, device_id=at_y(d), device_id_type=MESH)
    for d in x_far_first:
        pl.semaphore_signal(barrier, inc=1, device_id=at_x(d), device_id_type=MESH)
    pl.semaphore_signal(barrier, inc=1, device_id=sibling, device_id_type=MESH)

    def load(src, dst, index):
        copy = pltpu.make_async_copy(src, dst, in_sem.at[index])
        copy.start()
        return copy

    load_x = load(below_hbm, xb.at[pl.ds(2, 23)], 0)
    load_u1 = load(u_hbm.at[1], u.at[1], 1)
    load_rhs = load(rhs_hbm, rhs, 2)
    load_piv = load(piv_hbm, piv, 3)
    load_inv = load(inv_hbm, inv, 4)
    load_u0 = load(u_hbm.at[0], u.at[0], 5)
    load_uc = load(uc_hbm, uc, 6)
    load_rc = load(rc_hbm, rc, 7)
    load_map = load(map_hbm, cmap, 8)
    load_cnt = load(cnt_hbm, cnt, 9)

    def push(src, dst, phase, device):
        pltpu.make_async_remote_copy(
            src_ref=src, dst_ref=dst, send_sem=send.at[phase], recv_sem=recv.at[phase],
            device_id=device, device_id_type=MESH,
        ).start()

    def arrived(ref, phase):
        pltpu.make_async_remote_copy(
            src_ref=ref, dst_ref=ref, send_sem=send.at[phase], recv_sem=recv.at[phase],
            device_id=sibling, device_id_type=MESH,
        ).wait_recv()

    def sent(ref, phase):
        pltpu.make_async_remote_copy(
            src_ref=ref, dst_ref=ref, send_sem=send.at[phase], recv_sem=recv.at[phase],
            device_id=sibling, device_id_type=MESH,
        ).wait_send()

    xb[0] = jnp.zeros(xb.shape[1:], BF16)
    xb[1] = jnp.zeros(xb.shape[1:], BF16)

    def below_sum(panel):
        total = dot(xb[2], u[panel, 2], NT)
        for q in range(3, 25, 2):
            total += dot(
                jnp.concatenate([xb[q], xb[q + 1]], axis=1),
                jnp.concatenate([u[panel, q], u[panel, q + 1]], axis=1),
                NT,
            )
        return total

    load_x.wait()
    load_u1.wait()
    s1 = below_sum(1)
    p1a[...] = jnp.concatenate([s1[:16], s1[16:]], axis=1)
    pl.semaphore_wait(barrier, 2 * len(z_far_first) + len(y_far_first) + len(x_far_first) + 1)

    push(p1a, p1r, 0, sibling)
    load_rhs.wait()
    load_piv.wait()
    load_inv.wait()
    y1 = rhs[:, 1, :] * piv[1:2, :]
    y0 = rhs[:, 0, :] * piv[0:1, :]
    arrived(p1r, 0)
    chip = p1a[...] + p1r[...]
    p1s[...] = chip
    p1z[z] = chip
    for d in z_far_first:
        push(p1s, p1z.at[z], 1, at_z(d))

    load_u0.wait()
    for d in x_far_first:
        push(u.at[0, 1], l10g.at[d], 2, at_x(d))
        push(inv.at[0], m0g.at[d], 3, at_x(d))
    l10g[0] = u[0, 1]
    m0g[0] = inv[0]
    s0 = below_sum(0)
    sy_send[...] = jnp.concatenate([s0, y0], axis=1)
    for d in x_far_first:
        start = pl.multiple_of(lax.rem(xx + d, XS) * 8, 8)
        push(sy_send.at[pl.ds(start, 8)], sy_recv.at[d], 4, at_x(d))
    sy_recv[0] = sy_send[pl.ds(pl.multiple_of(xx * 8, 8), 8), :]
    load_uc.wait()
    ucf[...] = uc[...].astype(F32).reshape(ucf.shape)
    for d in range(16):
        ct[d] = ucf[pl.ds(d, 128, stride=16), :].astype(BF16)
    cr[0] = ct[0]

    arrived(p1z.at[pl.ds(0, 7)], 1)
    s1 = p1z[0]
    for k in range(1, ZS):
        s1 += p1z[k]
    s1 = jnp.concatenate([s1[:, :64], s1[:, 64:]], axis=0)
    t1 = (y1 - s1).astype(BF16)
    x1p[...] = dot(t1, inv[1], NN)
    for d in x_far_first:
        start = pl.multiple_of(lax.rem(xx + d, XS) * 8, 8)
        push(x1p.at[pl.ds(start, 8)], p2.at[xx], 5, at_x(d))
    p2[xx] = x1p[pl.ds(pl.multiple_of(xx * 8, 8), 8), :]
    for d in range(1, 16):
        push(ct.at[d], cr.at[d], 6, at_row(d))
    arrived(p2.at[pl.ds(0, 3)], 5)
    part = p2[0] + p2[1] + p2[2] + p2[3]
    p3s[...] = part
    p3[yy] = part
    for d in y_far_first:
        push(p3s, p3.at[yy], 7, at_y(d))

    arrived(sy_recv.at[pl.ds(1, 3)], 4)
    arrived(l10g.at[pl.ds(1, 3)], 2)
    below0 = jnp.concatenate([sy_recv[j][:, :64] for j in range(4)], axis=1)
    x0y[...] = jnp.concatenate([sy_recv[j][:, 64:] for j in range(4)], axis=1)
    l10 = l10g[...].reshape(256, 128)

    arrived(p3.at[pl.ds(0, 7)], 7)
    x1 = p3[0]
    for k in range(1, YS):
        x1 += p3[k]
    mine = pl.ds(pl.multiple_of(xx * 8, 8), 8)
    x_out[1, mine, :] = x1
    s0 = below0 + dot(x1.astype(BF16), l10, NT)
    p4a[pl.ds(0, 8), :] = s0[:, :128]
    p4a[pl.ds(8, 8), :] = s0[:, 128:]
    push(p4a, p4r, 8, sibling)
    for d in x_far_first:
        push(x_out.at[1, mine], x_out.at[1, mine], 9, at_x(d))
    arrived(m0g.at[pl.ds(1, 3)], 3)
    m0 = m0g[...].reshape(256, 128)
    arrived(p4r, 8)
    chip = p4a[...] + p4r[...]
    p4s[...] = chip
    p4z[z] = chip
    for d in z_far_first:
        push(p4s, p4z.at[z], 10, at_z(d))

    load_map.wait()
    load_cnt.wait()
    load_rc.wait()
    child = col // (XS * YS // 2)
    arrived(x_out.at[1, pl.ds(0, 24)], 9)

    arrived(p4z.at[pl.ds(0, 7)], 10)
    s0 = p4z[0]
    for k in range(1, ZS):
        s0 += p4z[k]
    t0 = (x0y[...] - jnp.concatenate([s0[:8], s0[8:]], axis=1)).astype(BF16)
    part = dot(t0, m0, NN)
    p5s[...] = part
    p5[yy] = part
    for d in y_far_first:
        push(p5s, p5.at[yy], 11, at_y(d))

    arrived(cr.at[pl.ds(1, 15)], 6)
    total = jnp.zeros((32, 128), F32)
    w0 = jnp.zeros((128, 128), F32)
    w1 = jnp.zeros((128, 128), F32)
    for d in range(16):
        slot = d * 16 + lax.rem(row - d + 16, 16)
        block = cmap[child, slot] // ROWS
        live = slot < cnt[child]
        weight = cr[d]
        term = dot(xb[block], weight, NT)
        total += jnp.where(live, term, 0.0)
        weight = weight.astype(F32)
        w0 += jnp.where(jnp.logical_and(live, block == 0), weight, 0.0)
        w1 += jnp.where(jnp.logical_and(live, block == 1), weight, 0.0)
    total += dot(x_out[1].astype(BF16), w1.astype(BF16), NT)
    w0 = w0.astype(BF16)

    arrived(p5.at[pl.ds(0, 7)], 11)
    x0 = p5[0]
    for k in range(1, YS):
        x0 += p5[k]
    x_out[0, mine, :] = x0
    for d in x_far_first:
        push(x_out.at[0, mine], x_out.at[0, mine], 12, at_x(d))
    arrived(x_out.at[0, pl.ds(0, 24)], 12)
    total += dot(x_out[0].astype(BF16), w0, NT)
    p7a[...] = total
    push(p7a, p7r, 13, sibling)
    arrived(p7r, 13)
    chip = p7a[...] + p7r[...]
    p7s[...] = chip
    p7z[z] = chip
    for d in z_far_first:
        push(p7s, p7z.at[z], 14, at_z(d))

    sent(p1a, 0)
    sent(p1z.at[pl.ds(0, 7)], 1)
    sent(l10g.at[pl.ds(1, 3)], 2)
    sent(m0g.at[pl.ds(1, 3)], 3)
    sent(sy_recv.at[pl.ds(1, 3)], 4)
    sent(p2.at[pl.ds(0, 3)], 5)
    sent(cr.at[pl.ds(1, 15)], 6)
    sent(p3.at[pl.ds(0, 7)], 7)
    sent(p4a, 8)
    sent(x_out.at[1, pl.ds(0, 24)], 9)
    sent(p4z.at[pl.ds(0, 7)], 10)
    sent(p5.at[pl.ds(0, 7)], 11)
    sent(x_out.at[0, pl.ds(0, 24)], 12)
    sent(p7a, 13)

    arrived(p7z.at[pl.ds(0, 7)], 14)
    total = p7z[0]
    for k in range(1, ZS):
        total += p7z[k]
    c_out[...] = rc[...] - total
    sent(p7z.at[pl.ds(0, 7)], 14)


def local(
    u_front,
    inverse_blocks,
    rhs_window,
    pivot_inverse,
    below_solution,
    u_child,
    rhs_child,
    child_map,
    child_counts,
):
    u = jnp.transpose(u_front, (0, 2, 1, 3))
    inv = jnp.transpose(inverse_blocks, (0, 2, 1, 3)).reshape(2, 64, 128)
    below = jnp.transpose(below_solution, (1, 0, 2))
    vm = pltpu.VMEM
    x, c = pl.pallas_call(
        kernel,
        out_shape=(
            jax.ShapeDtypeStruct((2, 32, 128), F32),
            jax.ShapeDtypeStruct((32, 128), F32),
        ),
        in_specs=[pl.BlockSpec(memory_space=pl.ANY)] * 9,
        out_specs=(pl.BlockSpec(memory_space=vm), pl.BlockSpec(memory_space=vm)),
        scratch_shapes=[
            vm((2, 25, 64, 128), BF16),
            vm((2, 64, 128), BF16),
            vm((32, 2, 64), F32),
            vm((2, 64), F32),
            vm((25, 32, 128), BF16),
            vm((128, 16, 128), BF16),
            vm((32, 128), F32),
            pltpu.SMEM((2, 256), jnp.int32),
            pltpu.SMEM((2,), jnp.int32),
            vm((2048, 128), F32),
            vm((16, 128, 128), BF16),
            vm((16, 128, 128), BF16),
            vm((2, 128, 128), BF16),
            vm((32, 128), F32),
            vm((4, 64, 128), BF16),
            vm((4, 64, 128), BF16),
            vm((32, 128), F32),
            vm((4, 8, 128), F32),
            vm((8, 256), F32),
            vm((16, 128), F32),
            vm((16, 128), F32),
            vm((16, 128), F32),
            vm((8, 16, 128), F32),
            vm((32, 128), F32),
            vm((4, 8, 128), F32),
            vm((8, 128), F32),
            vm((8, 8, 128), F32),
            vm((16, 128), F32),
            vm((16, 128), F32),
            vm((16, 128), F32),
            vm((8, 16, 128), F32),
            vm((8, 128), F32),
            vm((8, 8, 128), F32),
            vm((32, 128), F32),
            vm((32, 128), F32),
            vm((32, 128), F32),
            vm((8, 32, 128), F32),
            pltpu.SemaphoreType.DMA((10,)),
            pltpu.SemaphoreType.DMA((15,)),
            pltpu.SemaphoreType.DMA((15,)),
        ],
        compiler_params=pltpu.CompilerParams(
            collective_id=0, has_side_effects=True, vmem_limit_bytes=60 << 20
        ),
        name="solve",
    )(u, inv, rhs_window, pivot_inverse, below, u_child, rhs_child, child_map, child_counts)
    return jnp.transpose(x, (1, 0, 2)), c


def solution(mesh):
    return jax.shard_map(
        local,
        mesh=mesh,
        in_specs=(
            P(None, "col", None, "row"),
            P(None, "col", None, "row"),
            P(None, None, "col"),
            P(None, "col"),
            P(None, None, "row"),
            P("col", None, "row"),
            P(None, "col"),
            P(),
            P(),
        ),
        out_specs=(P(None, None, "row"), P(None, "col")),
        check_vma=False,
    )
```

```python
import functools

import jax
import jax.numpy as jnp
from jax import lax
from jax.experimental import pallas as pl
from jax.experimental.pallas import tpu as pltpu
from jax.sharding import PartitionSpec as P

MESH = pl.DeviceIdType.MESH
F32 = jnp.float32
BF16 = jnp.bfloat16
CORES = 2
ZS = 8
XS = 4
YS = 8
ROWS = ZS * CORES
NT = (((1,), (1,)), ((), ()))
NN = (((1,), (0,)), ((), ()))


def dot(a, b, dims):
    return lax.dot_general(a, b, dims, preferred_element_type=F32)


def kernel(
    u_hbm, inv_hbm, rhs_hbm, piv_hbm, below_hbm, uc_hbm, rc_hbm, map_hbm, cnt_hbm,
    x_out, c_out,
    u, inv, rhs, piv, xb, uc, rc, cmap, cnt,
    ucf, ct, cr, xfull,
    m1g, l10g, m0g, w0s, w0g, ys, yg,
    p1s, p1r,
    p3s, p3, p4s, p4, p5s, p5,
    p6a, p6r, p6s, p6z, p7s, p7,
    in_sem, send, recv,
):
    row = lax.axis_index("row")
    col = lax.axis_index("col")
    z = row // CORES
    core = lax.rem(row, CORES)
    xx = col // YS
    yy = lax.rem(col, YS)

    def at_row(d):
        return (lax.rem(row + d, ROWS), col)

    def at_z(d):
        return (lax.rem(z + d, ZS) * CORES + core, col)

    def at_x(d):
        return (row, lax.rem(xx + d, XS) * YS + yy)

    def at_y(d):
        return (row, xx * YS + lax.rem(yy + d, YS))

    def at_row_x(dr, dx):
        return (lax.rem(row + dr, ROWS), lax.rem(xx + dx, XS) * YS + yy)

    sibling = (z * CORES + (1 - core), col)
    z_far = (4, 3, 5, 2, 6, 1, 7)
    y_far = (4, 3, 5, 2, 6, 1, 7)
    x_far = (2, 1, 3)
    row_far = (8, 9, 7, 10, 6, 11, 5, 12, 4, 13, 3, 14, 2, 15, 1)
    row_x_far = [(dr, dx) for dx in (2, 1, 3) for dr in row_far + (0,)] + [(dr, 0) for dr in row_far]

    def load(src, dst, index):
        copy = pltpu.make_async_copy(src, dst, in_sem.at[index])
        copy.start()
        return copy

    barrier = pltpu.get_barrier_semaphore()

    def greet(device):
        pl.semaphore_signal(barrier, inc=1, device_id=device, device_id_type=MESH)

    load_x = load(below_hbm, xb.at[pl.ds(2, 23)], 0)
    load_u1 = load(u_hbm.at[1], u.at[1], 1)
    for dr, dx in row_x_far:
        greet(at_row_x(dr, dx))
    for d in y_far:
        greet(at_y(d))
    load_inv = load(inv_hbm, inv, 4)
    load_rhs = load(rhs_hbm, rhs, 2)
    load_piv = load(piv_hbm, piv, 3)
    load_u0 = load(u_hbm.at[0], u.at[0], 5)
    load_uc = load(uc_hbm, uc, 6)
    load_rc = load(rc_hbm, rc, 7)
    load_map = load(map_hbm, cmap, 8)
    load_cnt = load(cnt_hbm, cnt, 9)

    def push(src, dst, phase, device):
        pltpu.make_async_remote_copy(
            src_ref=src, dst_ref=dst, send_sem=send.at[phase], recv_sem=recv.at[phase],
            device_id=device, device_id_type=MESH,
        ).start()

    def whole(ref, phase):
        return pltpu.make_async_remote_copy(
            src_ref=ref, dst_ref=ref, send_sem=send.at[phase], recv_sem=recv.at[phase],
            device_id=sibling, device_id_type=MESH,
        )

    xb[0] = jnp.zeros(xb.shape[1:], BF16)
    xb[1] = jnp.zeros(xb.shape[1:], BF16)

    def below_sum(panel):
        total = dot(xb[2], u[panel, 2], NT)
        for q in range(3, 25, 2):
            total += dot(
                jnp.concatenate([xb[q], xb[q + 1]], axis=1),
                jnp.concatenate([u[panel, q], u[panel, q + 1]], axis=1),
                NT,
            )
        return total

    load_x.wait()
    load_u1.wait()
    s1 = below_sum(1)
    load_u0.wait()
    s0 = below_sum(0)
    p1s[...] = jnp.concatenate([s1, s0], axis=1).astype(BF16).reshape(4, 8, 128)
    load_rhs.wait()
    load_piv.wait()
    load_inv.wait()
    ys[...] = jnp.concatenate([rhs[:, 1, :] * piv[1:2, :], rhs[:, 0, :] * piv[0:1, :]], axis=1)
    pl.semaphore_wait(barrier, len(row_x_far) + len(y_far))
    for dr, dx in row_x_far:
        push(p1s.at[lax.rem(xx + dx, XS)], p1r.at[dx * ROWS + row], 0, at_row_x(dr, dx))
    p1r[row] = p1s[xx]
    for d in x_far:
        push(inv.at[1], m1g.at[d], 1, at_x(d))
    for d in x_far:
        start = pl.multiple_of(lax.rem(xx + d, XS) * 8, 8)
        push(ys.at[pl.ds(start, 8)], yg.at[d], 2, at_x(d))
    mine = pl.ds(pl.multiple_of(xx * 8, 8), 8)
    m1g[0] = inv[1]
    yg[0] = ys[mine, :]

    for d in x_far:
        push(u.at[0, 1], l10g.at[d], 4, at_x(d))
    for d in x_far:
        push(inv.at[0], m0g.at[d], 5, at_x(d))
    l10g[0] = u[0, 1]
    m0g[0] = inv[0]
    load_uc.wait()
    ucf[...] = uc[...].astype(F32).reshape(ucf.shape)
    for d in range(16):
        ct[d] = ucf[pl.ds(d, 128, stride=16), :].astype(BF16)
    cr[0] = ct[0]
    for d in row_far:
        push(ct.at[d], cr.at[d], 7, at_row(d))
    whole(yg.at[pl.ds(1, 3)], 2).wait_recv()
    y1 = jnp.concatenate([yg[j][:, :64] for j in range(XS)], axis=1)
    y0 = jnp.concatenate([yg[j][:, 64:] for j in range(XS)], axis=1)
    whole(m1g.at[pl.ds(1, 3)], 1).wait_recv()

    whole(p1r.at[pl.ds(0, 63)], 0).wait_recv()
    below = []
    for j in range(XS):
        total = p1r[j * ROWS].astype(F32)
        for k in range(1, ROWS):
            total += p1r[j * ROWS + k].astype(F32)
        below.append(total)
    t1 = (y1 - jnp.concatenate([v[:, :64] for v in below], axis=1)).astype(BF16)
    part = dot(t1, m1g[...].reshape(256, 128), NN)
    p3s[...] = part
    p3[yy] = part
    for d in y_far:
        push(p3s, p3.at[yy], 6, at_y(d))
    y0 = y0 - jnp.concatenate([v[:, 64:] for v in below], axis=1)
    whole(l10g.at[pl.ds(1, 3)], 4).wait_recv()
    whole(m0g.at[pl.ds(1, 3)], 5).wait_recv()

    whole(p3.at[pl.ds(0, 7)], 6).wait_recv()
    x1 = p3[0]
    for k in range(1, YS):
        x1 += p3[k]
    xfull[1, mine, :] = x1
    s0 = dot(x1.astype(BF16), l10g[...].reshape(256, 128), NT).astype(BF16)
    p4s[pl.ds(0, 8), :] = s0[:, :128]
    p4s[pl.ds(8, 8), :] = s0[:, 128:]
    for d in row_far:
        push(p4s, p4.at[row], 8, at_row(d))
    p4[row] = p4s[...]
    for d in x_far:
        push(xfull.at[1, mine], xfull.at[1, mine], 9, at_x(d))

    load_map.wait()
    load_cnt.wait()
    load_rc.wait()
    child = col // (XS * YS // 2)
    whole(cr.at[pl.ds(1, 15)], 7).wait_recv()
    w0 = jnp.zeros((128, 128), F32)
    for d in range(16):
        slot = d * 16 + lax.rem(row - d + 16, 16)
        wanted = jnp.logical_and(slot < cnt[child], cmap[child, slot] // ROWS == 0)
        w0 += jnp.where(wanted, cr[d].astype(F32), 0.0)
    w0s[...] = w0.astype(BF16)
    w0g[0] = w0s[...]
    for d in x_far:
        push(w0s, w0g.at[d], 10, at_x(d))

    whole(p4.at[pl.ds(0, 15)], 8).wait_recv()
    s0 = p4[0].astype(F32)
    for k in range(1, ROWS):
        s0 += p4[k].astype(F32)
    t0 = (y0 - jnp.concatenate([s0[:8], s0[8:]], axis=1)).astype(BF16)
    part = dot(t0, m0g[...].reshape(256, 128), NN)
    p5s[...] = part
    p5[yy] = part
    for d in y_far:
        push(p5s, p5.at[yy], 11, at_y(d))

    whole(xfull.at[1, pl.ds(0, 24)], 9).wait_recv()
    x1 = xfull[1]
    x_out[:, 1, :] = x1
    xb[1] = x1.astype(BF16)
    total = jnp.zeros((32, 128), F32)
    for d in range(16):
        slot = d * 16 + lax.rem(row - d + 16, 16)
        term = dot(xb[cmap[child, slot] // ROWS], cr[d], NT)
        total += jnp.where(slot < cnt[child], term, 0.0)
    p6a[...] = total
    push(p6a, p6r, 12, sibling)
    whole(w0g.at[pl.ds(1, 3)], 10).wait_recv()
    whole(p6r, 12).wait_recv()
    chip = (p6a[...] + p6r[...]).astype(BF16)
    p6s[...] = chip
    p6z[z] = chip
    for d in z_far:
        push(p6s, p6z.at[z], 13, at_z(d))

    whole(p5.at[pl.ds(0, 7)], 11).wait_recv()
    x0 = p5[0]
    for k in range(1, YS):
        x0 += p5[k]
    late = dot(x0.astype(BF16), w0g[...].reshape(512, 128), NT).astype(BF16)
    for j in range(XS):
        p7s[j] = late[:, 128 * j:128 * j + 128]
    for dr, dx in row_x_far:
        push(p7s.at[(XS - dx) % XS], p7.at[xx * ROWS + row], 14, at_row_x(dr, dx))
    p7[xx * ROWS + row] = p7s[0]
    xfull[0, mine, :] = x0
    for d in x_far:
        push(xfull.at[0, mine], xfull.at[0, mine], 15, at_x(d))

    whole(p1r.at[pl.ds(0, 63)], 0).wait_send()
    whole(m1g.at[pl.ds(1, 3)], 1).wait_send()
    whole(yg.at[pl.ds(1, 3)], 2).wait_send()
    whole(l10g.at[pl.ds(1, 3)], 4).wait_send()
    whole(m0g.at[pl.ds(1, 3)], 5).wait_send()
    whole(p3.at[pl.ds(0, 7)], 6).wait_send()
    whole(cr.at[pl.ds(1, 15)], 7).wait_send()
    whole(p4.at[pl.ds(0, 15)], 8).wait_send()
    whole(xfull.at[1, pl.ds(0, 24)], 9).wait_send()
    whole(w0g.at[pl.ds(1, 3)], 10).wait_send()
    whole(p5.at[pl.ds(0, 7)], 11).wait_send()
    whole(p6r, 12).wait_send()
    whole(p6z.at[pl.ds(0, 7)], 13).wait_send()

    whole(p6z.at[pl.ds(0, 7)], 13).wait_recv()
    total = p6z[0].astype(F32)
    for k in range(1, ZS):
        total += p6z[k].astype(F32)
    total = rc[...] - total
    whole(xfull.at[0, pl.ds(0, 24)], 15).wait()
    x_out[:, 0, :] = xfull[0]

    whole(p7.at[pl.ds(0, 63)], 14).wait()
    for j in range(XS):
        late = p7[j * ROWS].astype(F32)
        for k in range(1, ROWS):
            late += p7[j * ROWS + k].astype(F32)
        c_out[pl.ds(8 * j, 8), :] = total[8 * j:8 * j + 8] - late


def local(
    u_front,
    inverse_blocks,
    rhs_window,
    pivot_inverse,
    below_solution,
    u_child,
    rhs_child,
    child_map,
    child_counts,
):
    u = jnp.transpose(u_front, (0, 2, 1, 3))
    inv = jnp.transpose(inverse_blocks, (0, 2, 1, 3)).reshape(2, 64, 128)
    below = jnp.transpose(below_solution, (1, 0, 2))
    vm = pltpu.VMEM
    return pl.pallas_call(
        kernel,
        out_shape=(
            jax.ShapeDtypeStruct((32, 2, 128), F32),
            jax.ShapeDtypeStruct((32, 128), F32),
        ),
        in_specs=[pl.BlockSpec(memory_space=pl.ANY)] * 9,
        out_specs=(pl.BlockSpec(memory_space=vm), pl.BlockSpec(memory_space=vm)),
        scratch_shapes=[
            vm((2, 25, 64, 128), BF16),
            vm((2, 64, 128), BF16),
            vm((32, 2, 64), F32),
            vm((2, 64), F32),
            vm((25, 32, 128), BF16),
            vm((128, 16, 128), BF16),
            vm((32, 128), F32),
            pltpu.SMEM((2, 256), jnp.int32),
            pltpu.SMEM((2,), jnp.int32),
            vm((2048, 128), F32),
            vm((16, 128, 128), BF16),
            vm((16, 128, 128), BF16),
            vm((2, 32, 128), F32),
            vm((4, 64, 128), BF16),
            vm((4, 64, 128), BF16),
            vm((4, 64, 128), BF16),
            vm((128, 128), BF16),
            vm((4, 128, 128), BF16),
            vm((32, 128), F32),
            vm((4, 8, 128), F32),
            vm((4, 8, 128), BF16),
            vm((64, 8, 128), BF16),
            vm((8, 128), F32),
            vm((8, 8, 128), F32),
            vm((16, 128), BF16),
            vm((16, 16, 128), BF16),
            vm((8, 128), F32),
            vm((8, 8, 128), F32),
            vm((32, 128), F32),
            vm((32, 128), F32),
            vm((32, 128), BF16),
            vm((8, 32, 128), BF16),
            vm((4, 8, 128), BF16),
            vm((64, 8, 128), BF16),
            pltpu.SemaphoreType.DMA((10,)),
            pltpu.SemaphoreType.DMA((16,)),
            pltpu.SemaphoreType.DMA((16,)),
        ],
        compiler_params=pltpu.CompilerParams(
            collective_id=0, has_side_effects=True, vmem_limit_bytes=60 << 20
        ),
        name="solve",
    )(u, inv, rhs_window, pivot_inverse, below, u_child, rhs_child, child_map, child_counts)


def solution(mesh):
    return jax.shard_map(
        local,
        mesh=mesh,
        in_specs=(
            P(None, "col", None, "row"),
            P(None, "col", None, "row"),
            P(None, None, "col"),
            P(None, "col"),
            P(None, None, "row"),
            P("col", None, "row"),
            P(None, "col"),
            P(),
            P(),
        ),
        out_specs=(P(None, None, "row"), P(None, "col")),
        check_vma=False,
    )
```

```python
import functools

import jax
import jax.numpy as jnp
from jax import lax
from jax.experimental import pallas as pl
from jax.experimental.pallas import tpu as pltpu
from jax.sharding import PartitionSpec as P

MESH = pl.DeviceIdType.MESH
F32 = jnp.float32
BF16 = jnp.bfloat16
CORES = 2
ZS = 8
XS = 4
YS = 8
ROWS = ZS * CORES
NT = (((1,), (1,)), ((), ()))
NN = (((1,), (0,)), ((), ()))


def dot(a, b, dims):
    return lax.dot_general(a, b, dims, preferred_element_type=F32)


def kernel(
    u_hbm, inv_hbm, rhs_hbm, piv_hbm, below_hbm, uc_hbm, rc_hbm, map_hbm, cnt_hbm,
    x_out, c_out,
    u, inv, rhs, piv, xb, uc, rc, cmap, cnt,
    ucf, ct, cr, xfull,
    m1g, l10g, m0g, w0s, w0g, ys, yg, ss, sg,
    p1s, p1r,
    p3s, p3, p4s, p4, p5s, p5,
    p6a, p6r, p6s, p6z, p7s, p7,
    in_sem, send, recv,
):
    row = lax.axis_index("row")
    col = lax.axis_index("col")
    z = row // CORES
    core = lax.rem(row, CORES)
    xx = col // YS
    yy = lax.rem(col, YS)

    def at_row(d):
        return (lax.rem(row + d, ROWS), col)

    def at_z(d):
        return (lax.rem(z + d, ZS) * CORES + core, col)

    def at_x(d):
        return (row, lax.rem(xx + d, XS) * YS + yy)

    def at_y(d):
        return (row, xx * YS + lax.rem(yy + d, YS))

    def at_row_x(dr, dx):
        return (lax.rem(row + dr, ROWS), lax.rem(xx + dx, XS) * YS + yy)

    sibling = (z * CORES + (1 - core), col)
    z_far = (4, 3, 5, 2, 6, 1, 7)
    y_far = (4, 3, 5, 2, 6, 1, 7)
    x_far = (2, 1, 3)
    row_far = (8, 9, 7, 10, 6, 11, 5, 12, 4, 13, 3, 14, 2, 15, 1)
    row_x_far = [(dr, dx) for dx in (2, 1, 3) for dr in row_far + (0,)] + [(dr, 0) for dr in row_far]

    def load(src, dst, index):
        copy = pltpu.make_async_copy(src, dst, in_sem.at[index])
        copy.start()
        return copy

    barrier = pltpu.get_barrier_semaphore()

    def greet(device):
        pl.semaphore_signal(barrier, inc=1, device_id=device, device_id_type=MESH)

    load_x = load(below_hbm, xb.at[pl.ds(2, 23)], 0)
    load_u1 = load(u_hbm.at[1], u.at[1], 1)
    for dr, dx in row_x_far:
        greet(at_row_x(dr, dx))
    for d in y_far:
        greet(at_y(d))
    load_inv = load(inv_hbm, inv, 4)
    load_rhs = load(rhs_hbm, rhs, 2)
    load_piv = load(piv_hbm, piv, 3)
    load_u0 = load(u_hbm.at[0], u.at[0], 5)
    load_uc = load(uc_hbm, uc, 6)
    load_rc = load(rc_hbm, rc, 7)
    load_map = load(map_hbm, cmap, 8)
    load_cnt = load(cnt_hbm, cnt, 9)

    def push(src, dst, phase, device):
        pltpu.make_async_remote_copy(
            src_ref=src, dst_ref=dst, send_sem=send.at[phase], recv_sem=recv.at[phase],
            device_id=device, device_id_type=MESH,
        ).start()

    def whole(ref, phase):
        return pltpu.make_async_remote_copy(
            src_ref=ref, dst_ref=ref, send_sem=send.at[phase], recv_sem=recv.at[phase],
            device_id=sibling, device_id_type=MESH,
        )

    xb[0] = jnp.zeros(xb.shape[1:], BF16)
    xb[1] = jnp.zeros(xb.shape[1:], BF16)

    def below_sum(panel):
        total = dot(xb[2], u[panel, 2], NT)
        for q in range(3, 25, 2):
            total += dot(
                jnp.concatenate([xb[q], xb[q + 1]], axis=1),
                jnp.concatenate([u[panel, q], u[panel, q + 1]], axis=1),
                NT,
            )
        return total

    load_x.wait()
    load_u1.wait()
    s1 = below_sum(1)
    for k in range(XS):
        p1s[k] = jnp.concatenate([s1[8 * k:8 * k + 4], s1[8 * k + 4:8 * k + 8]], axis=1).astype(BF16)
    load_rhs.wait()
    load_piv.wait()
    load_inv.wait()
    ys[...] = jnp.concatenate([rhs[:, 1, :] * piv[1:2, :], rhs[:, 0, :] * piv[0:1, :]], axis=1)
    pl.semaphore_wait(barrier, len(row_x_far) + len(y_far))
    for dr, dx in row_x_far:
        push(p1s.at[lax.rem(xx + dx, XS)], p1r.at[dx * ROWS + row], 0, at_row_x(dr, dx))
    p1r[row] = p1s[xx]
    for d in x_far:
        push(inv.at[1], m1g.at[d], 1, at_x(d))
    for d in x_far:
        start = pl.multiple_of(lax.rem(xx + d, XS) * 8, 8)
        push(ys.at[pl.ds(start, 8)], yg.at[d], 2, at_x(d))
    mine = pl.ds(pl.multiple_of(xx * 8, 8), 8)
    m1g[0] = inv[1]
    yg[0] = ys[mine, :]

    load_uc.wait()
    ucf[...] = uc[...].astype(F32).reshape(ucf.shape)
    for d in range(16):
        ct[d] = ucf[pl.ds(d, 128, stride=16), :].astype(BF16)
    cr[0] = ct[0]
    for d in (5, 11, 6, 10, 7, 9, 8):
        push(ct.at[d], cr.at[d], 7, at_row(d))
    load_u0.wait()
    for d in x_far:
        push(u.at[0, 1], l10g.at[d], 4, at_x(d))
    for d in x_far:
        push(inv.at[0], m0g.at[d], 5, at_x(d))
    l10g[0] = u[0, 1]
    m0g[0] = inv[0]
    s0 = below_sum(0)
    ss[...] = jnp.concatenate([s0, s0], axis=1)
    for d in x_far:
        start = pl.multiple_of(lax.rem(xx + d, XS) * 8, 8)
        push(ss.at[pl.ds(start, 8)], sg.at[d], 3, at_x(d))
    sg[0] = ss[mine, :]
    whole(yg.at[pl.ds(1, 3)], 2).wait_recv()
    y1 = jnp.concatenate([yg[j][:, :64] for j in range(XS)], axis=1)
    y0 = jnp.concatenate([yg[j][:, 64:] for j in range(XS)], axis=1)
    whole(m1g.at[pl.ds(1, 3)], 1).wait_recv()

    whole(p1r.at[pl.ds(0, 63)], 0).wait_recv()
    sums = []
    for j in range(XS):
        total = p1r[j * ROWS].astype(F32)
        for k in range(1, ROWS):
            total += p1r[j * ROWS + k].astype(F32)
        sums.append(total)
    s1 = jnp.concatenate(
        [
            jnp.concatenate([v[:, :64] for v in sums], axis=1),
            jnp.concatenate([v[:, 64:] for v in sums], axis=1),
        ],
        axis=0,
    )
    t1 = (y1 - s1).astype(BF16)
    part = dot(t1, m1g[...].reshape(256, 128), NN)
    p3s[...] = part
    p3[yy] = part
    for d in y_far:
        push(p3s, p3.at[yy], 6, at_y(d))
    for d in (1, 15, 2, 14, 3, 13, 4, 12):
        push(ct.at[d], cr.at[d], 7, at_row(d))
    whole(sg.at[pl.ds(1, 3)], 3).wait_recv()
    below0 = jnp.concatenate([sg[j][:, :64] for j in range(XS)], axis=1)
    whole(l10g.at[pl.ds(1, 3)], 4).wait_recv()
    whole(m0g.at[pl.ds(1, 3)], 5).wait_recv()

    whole(p3.at[pl.ds(0, 7)], 6).wait_recv()
    x1 = p3[0]
    for k in range(1, YS):
        x1 += p3[k]
    xfull[1, mine, :] = x1
    s0 = (below0 + dot(x1.astype(BF16), l10g[...].reshape(256, 128), NT)).astype(BF16)
    p4s[pl.ds(0, 8), :] = s0[:, :128]
    p4s[pl.ds(8, 8), :] = s0[:, 128:]
    for d in row_far:
        push(p4s, p4.at[row], 8, at_row(d))
    p4[row] = p4s[...]
    for d in x_far:
        push(xfull.at[1, mine], xfull.at[1, mine], 9, at_x(d))

    load_map.wait()
    load_cnt.wait()
    load_rc.wait()
    child = col // (XS * YS // 2)
    whole(cr.at[pl.ds(1, 15)], 7).wait_recv()
    w0 = jnp.zeros((128, 128), F32)
    for d in range(16):
        slot = d * 16 + lax.rem(row - d + 16, 16)
        wanted = jnp.logical_and(slot < cnt[child], cmap[child, slot] // ROWS == 0)
        w0 += jnp.where(wanted, cr[d].astype(F32), 0.0)
    w0s[...] = w0.astype(BF16)
    w0g[0] = w0s[...]
    for d in x_far:
        push(w0s, w0g.at[d], 10, at_x(d))

    whole(p4.at[pl.ds(0, 15)], 8).wait_recv()
    s0 = p4[0].astype(F32)
    for k in range(1, ROWS):
        s0 += p4[k].astype(F32)
    t0 = (y0 - jnp.concatenate([s0[:8], s0[8:]], axis=1)).astype(BF16)
    part = dot(t0, m0g[...].reshape(256, 128), NN)
    p5s[...] = part
    p5[yy] = part
    for d in y_far:
        push(p5s, p5.at[yy], 11, at_y(d))

    whole(xfull.at[1, pl.ds(0, 24)], 9).wait_recv()
    x1 = xfull[1]
    x_out[:, 1, :] = x1
    xb[1] = x1.astype(BF16)
    total = jnp.zeros((32, 128), F32)
    for d in range(16):
        slot = d * 16 + lax.rem(row - d + 16, 16)
        term = dot(xb[cmap[child, slot] // ROWS], cr[d], NT)
        total += jnp.where(slot < cnt[child], term, 0.0)
    p6a[...] = total
    push(p6a, p6r, 12, sibling)
    whole(w0g.at[pl.ds(1, 3)], 10).wait_recv()
    whole(p6r, 12).wait_recv()
    chip = (p6a[...] + p6r[...]).astype(BF16)
    p6s[...] = chip
    p6z[z] = chip
    for d in z_far:
        push(p6s, p6z.at[z], 13, at_z(d))

    whole(p5.at[pl.ds(0, 7)], 11).wait_recv()
    x0 = p5[0]
    for k in range(1, YS):
        x0 += p5[k]
    late = dot(x0.astype(BF16), w0g[...].reshape(512, 128), NT).astype(BF16)
    for j in range(XS):
        p7s[j] = late[:, 128 * j:128 * j + 128]
    for dr, dx in row_x_far:
        push(p7s.at[(XS - dx) % XS], p7.at[xx * ROWS + row], 14, at_row_x(dr, dx))
    p7[xx * ROWS + row] = p7s[0]
    xfull[0, mine, :] = x0
    for d in x_far:
        push(xfull.at[0, mine], xfull.at[0, mine], 15, at_x(d))

    whole(p1r.at[pl.ds(0, 63)], 0).wait_send()
    whole(m1g.at[pl.ds(1, 3)], 1).wait_send()
    whole(yg.at[pl.ds(1, 3)], 2).wait_send()
    whole(sg.at[pl.ds(1, 3)], 3).wait_send()
    whole(l10g.at[pl.ds(1, 3)], 4).wait_send()
    whole(m0g.at[pl.ds(1, 3)], 5).wait_send()
    whole(p3.at[pl.ds(0, 7)], 6).wait_send()
    whole(cr.at[pl.ds(1, 15)], 7).wait_send()
    whole(p4.at[pl.ds(0, 15)], 8).wait_send()
    whole(xfull.at[1, pl.ds(0, 24)], 9).wait_send()
    whole(w0g.at[pl.ds(1, 3)], 10).wait_send()
    whole(p5.at[pl.ds(0, 7)], 11).wait_send()
    whole(p6r, 12).wait_send()
    whole(p6z.at[pl.ds(0, 7)], 13).wait_send()

    whole(p6z.at[pl.ds(0, 7)], 13).wait_recv()
    total = p6z[0].astype(F32)
    for k in range(1, ZS):
        total += p6z[k].astype(F32)
    total = rc[...] - total
    whole(xfull.at[0, pl.ds(0, 24)], 15).wait()
    x_out[:, 0, :] = xfull[0]

    whole(p7.at[pl.ds(0, 63)], 14).wait()
    for j in range(XS):
        late = p7[j * ROWS].astype(F32)
        for k in range(1, ROWS):
            late += p7[j * ROWS + k].astype(F32)
        c_out[pl.ds(8 * j, 8), :] = total[8 * j:8 * j + 8] - late


def local(
    u_front,
    inverse_blocks,
    rhs_window,
    pivot_inverse,
    below_solution,
    u_child,
    rhs_child,
    child_map,
    child_counts,
):
    u = jnp.transpose(u_front, (0, 2, 1, 3))
    inv = jnp.transpose(inverse_blocks, (0, 2, 1, 3)).reshape(2, 64, 128)
    below = jnp.transpose(below_solution, (1, 0, 2))
    vm = pltpu.VMEM
    return pl.pallas_call(
        kernel,
        out_shape=(
            jax.ShapeDtypeStruct((32, 2, 128), F32),
            jax.ShapeDtypeStruct((32, 128), F32),
        ),
        in_specs=[pl.BlockSpec(memory_space=pl.ANY)] * 9,
        out_specs=(pl.BlockSpec(memory_space=vm), pl.BlockSpec(memory_space=vm)),
        scratch_shapes=[
            vm((2, 25, 64, 128), BF16),
            vm((2, 64, 128), BF16),
            vm((32, 2, 64), F32),
            vm((2, 64), F32),
            vm((25, 32, 128), BF16),
            vm((128, 16, 128), BF16),
            vm((32, 128), F32),
            pltpu.SMEM((2, 256), jnp.int32),
            pltpu.SMEM((2,), jnp.int32),
            vm((2048, 128), F32),
            vm((16, 128, 128), BF16),
            vm((16, 128, 128), BF16),
            vm((2, 32, 128), F32),
            vm((4, 64, 128), BF16),
            vm((4, 64, 128), BF16),
            vm((4, 64, 128), BF16),
            vm((128, 128), BF16),
            vm((4, 128, 128), BF16),
            vm((32, 128), F32),
            vm((4, 8, 128), F32),
            vm((32, 128), F32),
            vm((4, 8, 128), F32),
            vm((4, 4, 128), BF16),
            vm((64, 4, 128), BF16),
            vm((8, 128), F32),
            vm((8, 8, 128), F32),
            vm((16, 128), BF16),
            vm((16, 16, 128), BF16),
            vm((8, 128), F32),
            vm((8, 8, 128), F32),
            vm((32, 128), F32),
            vm((32, 128), F32),
            vm((32, 128), BF16),
            vm((8, 32, 128), BF16),
            vm((4, 8, 128), BF16),
            vm((64, 8, 128), BF16),
            pltpu.SemaphoreType.DMA((10,)),
            pltpu.SemaphoreType.DMA((16,)),
            pltpu.SemaphoreType.DMA((16,)),
        ],
        compiler_params=pltpu.CompilerParams(
            collective_id=0, has_side_effects=True, vmem_limit_bytes=60 << 20
        ),
        name="solve",
    )(u, inv, rhs_window, pivot_inverse, below, u_child, rhs_child, child_map, child_counts)


def solution(mesh):
    return jax.shard_map(
        local,
        mesh=mesh,
        in_specs=(
            P(None, "col", None, "row"),
            P(None, "col", None, "row"),
            P(None, None, "col"),
            P(None, "col"),
            P(None, None, "row"),
            P("col", None, "row"),
            P(None, "col"),
            P(),
            P(),
        ),
        out_specs=(P(None, None, "row"), P(None, "col")),
        check_vma=False,
    )
```

```python
import functools

import jax
import jax.numpy as jnp
from jax import lax
from jax.experimental import pallas as pl
from jax.experimental.pallas import tpu as pltpu
from jax.sharding import PartitionSpec as P

MESH = pl.DeviceIdType.MESH
F32 = jnp.float32
BF16 = jnp.bfloat16
CORES = 2
ZS = 8
XS = 4
YS = 8
ROWS = ZS * CORES
NT = (((1,), (1,)), ((), ()))
NN = (((1,), (0,)), ((), ()))


def dot(a, b, dims):
    return lax.dot_general(a, b, dims, preferred_element_type=F32)


def kernel(
    u_hbm, inv_hbm, rhs_hbm, piv_hbm, below_hbm, uc_hbm, rc_hbm, map_hbm, cnt_hbm,
    x_out, c_out,
    u, inv, rhs, piv, xb, uc, rc, cmap, cnt,
    ucf, ct, cr, xfull,
    l10g, m0g, w0s, w0g, ss, sg,
    p1s, p1r,
    p3s, p3, p4s, p4, p5s, p5,
    p6a, p6r, p6s, p6z, p7s, p7,
    in_sem, send, recv, ready,
):
    row = lax.axis_index("row")
    col = lax.axis_index("col")
    z = row // CORES
    core = lax.rem(row, CORES)
    xx = col // YS
    yy = lax.rem(col, YS)

    def at_row(d):
        return (lax.rem(row + d, ROWS), col)

    def at_z(d):
        return (lax.rem(z + d, ZS) * CORES + core, col)

    def at_x(d):
        return (row, lax.rem(xx + d, XS) * YS + yy)

    def at_y(d):
        return (row, xx * YS + lax.rem(yy + d, YS))

    def at_row_x(dr, dx):
        return (lax.rem(row + dr, ROWS), lax.rem(xx + dx, XS) * YS + yy)

    def at_col(dx, dy):
        return (row, lax.rem(xx + dx, XS) * YS + lax.rem(yy + dy, YS))

    sibling = (z * CORES + (1 - core), col)
    z_far = (4, 3, 5, 2, 6, 1, 7)
    y_far = (4, 3, 5, 2, 6, 1, 7)
    x_far = (2, 1, 3)
    row_far = (8, 9, 7, 10, 6, 11, 5, 12, 4, 13, 3, 14, 2, 15, 1)
    col_far = [(dx, dy) for dx in (2, 1, 3) for dy in (4, 3, 5, 2, 6, 1, 7, 0)] + [(0, dy) for dy in (4, 3, 5, 2, 6, 1, 7)]
    row_x_far = [(dr, dx) for dx in (2, 1, 3) for dr in row_far + (0,)] + [(dr, 0) for dr in row_far]

    def load(src, dst, index):
        copy = pltpu.make_async_copy(src, dst, in_sem.at[index])
        copy.start()
        return copy

    barrier = pltpu.get_barrier_semaphore()

    def greet(device):
        pl.semaphore_signal(barrier, inc=1, device_id=device, device_id_type=MESH)

    load_x = load(below_hbm, xb.at[pl.ds(2, 23)], 0)
    load_u1 = load(u_hbm.at[1], u.at[1], 1)
    for d in row_far:
        greet(at_row(d))
    for d in y_far:
        greet(at_y(d))
    for d in x_far:
        greet(at_x(d))
    load_rhs = load(rhs_hbm, rhs, 2)
    load_piv = load(piv_hbm, piv, 3)
    load_inv = load(inv_hbm, inv, 4)
    load_u0 = load(u_hbm.at[0], u.at[0], 5)
    load_uc = load(uc_hbm, uc, 6)
    load_rc = load(rc_hbm, rc, 7)
    load_map = load(map_hbm, cmap, 8)
    load_cnt = load(cnt_hbm, cnt, 9)

    def push(src, dst, phase, device):
        pltpu.make_async_remote_copy(
            src_ref=src, dst_ref=dst, send_sem=send.at[phase], recv_sem=recv.at[phase],
            device_id=device, device_id_type=MESH,
        ).start()

    def whole(ref, phase):
        return pltpu.make_async_remote_copy(
            src_ref=ref, dst_ref=ref, send_sem=send.at[phase], recv_sem=recv.at[phase],
            device_id=sibling, device_id_type=MESH,
        )

    xb[0] = jnp.zeros(xb.shape[1:], BF16)
    xb[1] = jnp.zeros(xb.shape[1:], BF16)

    def below_sum(panel):
        total = dot(xb[2], u[panel, 2], NT)
        for q in range(3, 25, 2):
            total += dot(
                jnp.concatenate([xb[q], xb[q + 1]], axis=1),
                jnp.concatenate([u[panel, q], u[panel, q + 1]], axis=1),
                NT,
            )
        return total

    load_x.wait()
    load_u1.wait()
    s1 = below_sum(1)
    p1s[...] = jnp.concatenate([s1[:16], s1[16:]], axis=1).astype(BF16)
    pl.semaphore_wait(barrier, len(row_far) + len(y_far) + len(x_far))
    for d in row_far:
        push(p1s, p1r.at[row], 0, at_row(d))
    p1r[row] = p1s[...]
    for d in x_far:
        pl.semaphore_signal(ready, inc=1, device_id=at_x(d), device_id_type=MESH)
    load_rhs.wait()
    load_piv.wait()
    load_inv.wait()
    y1 = rhs[:, 1, :] * piv[1:2, :]
    y0 = rhs[:, 0, :] * piv[0:1, :]
    mine = pl.ds(pl.multiple_of(xx * 8, 8), 8)

    load_uc.wait()
    ucf[...] = uc[...].astype(F32).reshape(ucf.shape)
    for d in range(16):
        ct[d] = ucf[pl.ds(d, 128, stride=16), :].astype(BF16)
    cr[0] = ct[0]
    for d in (13, 4, 12, 5, 11, 6, 10, 7, 9, 8):
        push(ct.at[d], cr.at[d], 7, at_row(d))
    load_u0.wait()
    for d in x_far:
        push(u.at[0, 1], l10g.at[d], 4, at_x(d))
    for d in x_far:
        push(inv.at[0], m0g.at[d], 5, at_x(d))
    l10g[0] = u[0, 1]
    m0g[0] = inv[0]
    s0 = below_sum(0)
    ss[...] = jnp.concatenate([s0, y0], axis=1)
    for d in x_far:
        start = pl.multiple_of(lax.rem(xx + d, XS) * 8, 8)
        push(ss.at[pl.ds(start, 8)], sg.at[d], 3, at_x(d))
    sg[0] = ss[mine, :]
    pl.semaphore_wait(ready, len(x_far))

    whole(p1r.at[pl.ds(0, 15)], 0).wait_recv()
    s1 = p1r[0].astype(F32)
    for k in range(1, ROWS):
        s1 += p1r[k].astype(F32)
    s1 = jnp.concatenate([s1[:, :64], s1[:, 64:]], axis=0)
    part = dot((y1 - s1).astype(BF16), inv[1], NN).astype(p3s.dtype)
    p3s[...] = part.reshape(4, 8, 128)
    for dx, dy in col_far:
        push(p3s.at[lax.rem(xx + dx, XS)], p3.at[col], 6, at_col(dx, dy))
    p3[col] = p3s[xx]
    for d in (1, 15, 2, 14, 3):
        push(ct.at[d], cr.at[d], 7, at_row(d))
    whole(sg.at[pl.ds(1, 3)], 3).wait_recv()
    below0 = jnp.concatenate([sg[j][:, :64] for j in range(XS)], axis=1)
    y0 = jnp.concatenate([sg[j][:, 64:] for j in range(XS)], axis=1)
    whole(l10g.at[pl.ds(1, 3)], 4).wait_recv()
    whole(m0g.at[pl.ds(1, 3)], 5).wait_recv()

    whole(p3.at[pl.ds(0, 31)], 6).wait_recv()
    x1 = p3[0].astype(F32)
    for k in range(1, XS * YS):
        x1 += p3[k].astype(F32)
    xfull[1, mine, :] = x1
    s0 = (below0 + dot(x1.astype(BF16), l10g[...].reshape(256, 128), NT)).astype(BF16)
    p4s[pl.ds(0, 8), :] = s0[:, :128]
    p4s[pl.ds(8, 8), :] = s0[:, 128:]
    for d in row_far:
        push(p4s, p4.at[row], 8, at_row(d))
    p4[row] = p4s[...]
    for d in x_far:
        push(xfull.at[1, mine], xfull.at[1, mine], 9, at_x(d))

    load_map.wait()
    load_cnt.wait()
    load_rc.wait()
    child = col // (XS * YS // 2)
    whole(cr.at[pl.ds(1, 15)], 7).wait_recv()
    w0 = jnp.zeros((128, 128), F32)
    for d in range(16):
        slot = d * 16 + lax.rem(row - d + 16, 16)
        wanted = jnp.logical_and(slot < cnt[child], cmap[child, slot] // ROWS == 0)
        w0 += jnp.where(wanted, cr[d].astype(F32), 0.0)
    w0s[...] = w0.astype(BF16)
    w0g[0] = w0s[...]
    for d in x_far:
        push(w0s, w0g.at[d], 10, at_x(d))

    whole(p4.at[pl.ds(0, 15)], 8).wait_recv()
    s0 = p4[0].astype(F32)
    for k in range(1, ROWS):
        s0 += p4[k].astype(F32)
    t0 = (y0 - jnp.concatenate([s0[:8], s0[8:]], axis=1)).astype(BF16)
    part = dot(t0, m0g[...].reshape(256, 128), NN)
    p5s[...] = part
    p5[yy] = part
    for d in y_far:
        push(p5s, p5.at[yy], 11, at_y(d))

    whole(xfull.at[1, pl.ds(0, 24)], 9).wait_recv()
    x1 = xfull[1]
    x_out[:, 1, :] = x1
    xb[1] = x1.astype(BF16)
    total = jnp.zeros((32, 128), F32)
    for d in range(16):
        slot = d * 16 + lax.rem(row - d + 16, 16)
        term = dot(xb[cmap[child, slot] // ROWS], cr[d], NT)
        total += jnp.where(slot < cnt[child], term, 0.0)
    p6a[...] = total
    push(p6a, p6r, 12, sibling)
    whole(w0g.at[pl.ds(1, 3)], 10).wait_recv()
    whole(p6r, 12).wait_recv()
    chip = (p6a[...] + p6r[...]).astype(BF16)
    p6s[...] = chip
    p6z[z] = chip
    for d in z_far:
        push(p6s, p6z.at[z], 13, at_z(d))

    whole(p5.at[pl.ds(0, 7)], 11).wait_recv()
    x0 = p5[0]
    for k in range(1, YS):
        x0 += p5[k]
    late = dot(x0.astype(BF16), w0g[...].reshape(512, 128), NT).astype(BF16)
    for j in range(XS):
        p7s[j] = late[:, 128 * j:128 * j + 128]
    for dr, dx in row_x_far:
        push(p7s.at[(XS - dx) % XS], p7.at[xx * ROWS + row], 14, at_row_x(dr, dx))
    p7[xx * ROWS + row] = p7s[0]
    xfull[0, mine, :] = x0
    for d in x_far:
        push(xfull.at[0, mine], xfull.at[0, mine], 15, at_x(d))

    whole(p1r.at[pl.ds(0, 15)], 0).wait_send()
    whole(sg.at[pl.ds(1, 3)], 3).wait_send()
    whole(l10g.at[pl.ds(1, 3)], 4).wait_send()
    whole(m0g.at[pl.ds(1, 3)], 5).wait_send()
    whole(p3.at[pl.ds(0, 31)], 6).wait_send()
    whole(cr.at[pl.ds(1, 15)], 7).wait_send()
    whole(p4.at[pl.ds(0, 15)], 8).wait_send()
    whole(xfull.at[1, pl.ds(0, 24)], 9).wait_send()
    whole(w0g.at[pl.ds(1, 3)], 10).wait_send()
    whole(p5.at[pl.ds(0, 7)], 11).wait_send()
    whole(p6r, 12).wait_send()
    whole(p6z.at[pl.ds(0, 7)], 13).wait_send()

    whole(p6z.at[pl.ds(0, 7)], 13).wait_recv()
    total = p6z[0].astype(F32)
    for k in range(1, ZS):
        total += p6z[k].astype(F32)
    total = rc[...] - total
    whole(xfull.at[0, pl.ds(0, 24)], 15).wait()
    x_out[:, 0, :] = xfull[0]

    whole(p7.at[pl.ds(0, 63)], 14).wait()
    for j in range(XS):
        late = p7[j * ROWS].astype(F32)
        for k in range(1, ROWS):
            late += p7[j * ROWS + k].astype(F32)
        c_out[pl.ds(8 * j, 8), :] = total[8 * j:8 * j + 8] - late


def local(
    u_front,
    inverse_blocks,
    rhs_window,
    pivot_inverse,
    below_solution,
    u_child,
    rhs_child,
    child_map,
    child_counts,
):
    u = jnp.transpose(u_front, (0, 2, 1, 3))
    inv = jnp.transpose(inverse_blocks, (0, 2, 1, 3)).reshape(2, 64, 128)
    below = jnp.transpose(below_solution, (1, 0, 2))
    vm = pltpu.VMEM
    return pl.pallas_call(
        kernel,
        out_shape=(
            jax.ShapeDtypeStruct((32, 2, 128), F32),
            jax.ShapeDtypeStruct((32, 128), F32),
        ),
        in_specs=[pl.BlockSpec(memory_space=pl.ANY)] * 9,
        out_specs=(pl.BlockSpec(memory_space=vm), pl.BlockSpec(memory_space=vm)),
        scratch_shapes=[
            vm((2, 25, 64, 128), BF16),
            vm((2, 64, 128), BF16),
            vm((32, 2, 64), F32),
            vm((2, 64), F32),
            vm((25, 32, 128), BF16),
            vm((128, 16, 128), BF16),
            vm((32, 128), F32),
            pltpu.SMEM((2, 256), jnp.int32),
            pltpu.SMEM((2,), jnp.int32),
            vm((2048, 128), F32),
            vm((16, 128, 128), BF16),
            vm((16, 128, 128), BF16),
            vm((2, 32, 128), F32),
            vm((4, 64, 128), BF16),
            vm((4, 64, 128), BF16),
            vm((128, 128), BF16),
            vm((4, 128, 128), BF16),
            vm((32, 128), F32),
            vm((4, 8, 128), F32),
            vm((16, 128), BF16),
            vm((16, 16, 128), BF16),
            vm((4, 8, 128), F32),
            vm((32, 8, 128), F32),
            vm((16, 128), BF16),
            vm((16, 16, 128), BF16),
            vm((8, 128), F32),
            vm((8, 8, 128), F32),
            vm((32, 128), F32),
            vm((32, 128), F32),
            vm((32, 128), BF16),
            vm((8, 32, 128), BF16),
            vm((4, 8, 128), BF16),
            vm((64, 8, 128), BF16),
            pltpu.SemaphoreType.DMA((10,)),
            pltpu.SemaphoreType.DMA((16,)),
            pltpu.SemaphoreType.DMA((16,)),
            pltpu.SemaphoreType.REGULAR,
        ],
        compiler_params=pltpu.CompilerParams(
            collective_id=0, has_side_effects=True, vmem_limit_bytes=60 << 20
        ),
        name="solve",
    )(u, inv, rhs_window, pivot_inverse, below, u_child, rhs_child, child_map, child_counts)


def solution(mesh):
    return jax.shard_map(
        local,
        mesh=mesh,
        in_specs=(
            P(None, "col", None, "row"),
            P(None, "col", None, "row"),
            P(None, None, "col"),
            P(None, "col"),
            P(None, None, "row"),
            P("col", None, "row"),
            P(None, "col"),
            P(),
            P(),
        ),
        out_specs=(P(None, None, "row"), P(None, "col")),
        check_vma=False,
    )
```

```python
import functools

import jax
import jax.numpy as jnp
from jax import lax
from jax.experimental import pallas as pl
from jax.experimental.pallas import tpu as pltpu
from jax.sharding import PartitionSpec as P

MESH = pl.DeviceIdType.MESH
F32 = jnp.float32
BF16 = jnp.bfloat16
CORES = 2
ZS = 8
XS = 4
YS = 8
ROWS = ZS * CORES
NT = (((1,), (1,)), ((), ()))
NN = (((1,), (0,)), ((), ()))


def dot(a, b, dims):
    return lax.dot_general(a, b, dims, preferred_element_type=F32)


def kernel(
    u_hbm, inv_hbm, rhs_hbm, piv_hbm, below_hbm, uc_hbm, rc_hbm, map_hbm, cnt_hbm,
    x_hbm, c_hbm,
    u, inv, rhs, piv, xb, uc, rc, cmap, cnt,
    ucf, ct, cr, xfull,
    l10g, m0g, w0s, w0g, ss, sg,
    p1s, p1r,
    p3s, p3, p4s, p4, p5s, p5,
    p6s, p6, p7s, p7,
    x_out, c_out, in_sem, send, recv, ready,
):
    row = lax.axis_index("row")
    col = lax.axis_index("col")
    z = row // CORES
    core = lax.rem(row, CORES)
    xx = col // YS
    yy = lax.rem(col, YS)

    def at_row(d):
        return (lax.rem(row + d, ROWS), col)

    def at_x(d):
        return (row, lax.rem(xx + d, XS) * YS + yy)

    def at_y(d):
        return (row, xx * YS + lax.rem(yy + d, YS))

    def at_row_x(dr, dx):
        return (lax.rem(row + dr, ROWS), lax.rem(xx + dx, XS) * YS + yy)

    def at_col(dx, dy):
        return (row, lax.rem(xx + dx, XS) * YS + lax.rem(yy + dy, YS))

    sibling = (z * CORES + (1 - core), col)
    y_far = (4, 3, 5, 2, 6, 1, 7)
    x_far = (2, 1, 3)
    row_far = (8, 9, 7, 10, 6, 11, 5, 12, 4, 13, 3, 14, 2, 15, 1)
    col_far = [(dx, dy) for dx in (2, 1, 3) for dy in (4, 3, 5, 2, 6, 1, 7, 0)] + [(0, dy) for dy in (4, 3, 5, 2, 6, 1, 7)]
    row_x_far = [(dr, dx) for dx in (2, 1, 3) for dr in row_far + (0,)] + [(dr, 0) for dr in row_far]

    def load(src, dst, index):
        copy = pltpu.make_async_copy(src, dst, in_sem.at[index])
        copy.start()
        return copy

    barrier = pltpu.get_barrier_semaphore()

    def greet(device):
        pl.semaphore_signal(barrier, inc=1, device_id=device, device_id_type=MESH)

    load_x = load(below_hbm, xb.at[pl.ds(2, 23)], 0)
    load_u1 = load(u_hbm.at[1], u.at[1], 1)
    for d in row_far:
        greet(at_row(d))
    for d in y_far:
        greet(at_y(d))
    for d in x_far:
        greet(at_x(d))
    load_rhs = load(rhs_hbm, rhs, 2)
    load_piv = load(piv_hbm, piv, 3)
    load_inv = load(inv_hbm, inv, 4)
    load_u0 = load(u_hbm.at[0], u.at[0], 5)
    load_uc = load(uc_hbm, uc, 6)
    load_rc = load(rc_hbm, rc, 7)
    load_map = load(map_hbm, cmap, 8)
    load_cnt = load(cnt_hbm, cnt, 9)

    def push(src, dst, phase, device):
        pltpu.make_async_remote_copy(
            src_ref=src, dst_ref=dst, send_sem=send.at[phase], recv_sem=recv.at[phase],
            device_id=device, device_id_type=MESH,
        ).start()

    def whole(ref, phase):
        return pltpu.make_async_remote_copy(
            src_ref=ref, dst_ref=ref, send_sem=send.at[phase], recv_sem=recv.at[phase],
            device_id=sibling, device_id_type=MESH,
        )

    xb[0] = jnp.zeros(xb.shape[1:], BF16)
    xb[1] = jnp.zeros(xb.shape[1:], BF16)

    def below_sum(panel):
        total = dot(xb[2], u[panel, 2], NT)
        for q in range(3, 25, 2):
            total += dot(
                jnp.concatenate([xb[q], xb[q + 1]], axis=1),
                jnp.concatenate([u[panel, q], u[panel, q + 1]], axis=1),
                NT,
            )
        return total

    load_x.wait()
    load_u1.wait()
    s1 = below_sum(1)
    p1s[...] = jnp.concatenate([s1[:16], s1[16:]], axis=1).astype(BF16)
    pl.semaphore_wait(barrier, len(row_far) + len(y_far) + len(x_far))
    for d in row_far:
        push(p1s, p1r.at[row], 0, at_row(d))
    p1r[row] = p1s[...]
    for d in x_far:
        pl.semaphore_signal(ready, inc=1, device_id=at_x(d), device_id_type=MESH)
    load_rhs.wait()
    load_piv.wait()
    load_inv.wait()
    y1 = rhs[:, 1, :] * piv[1:2, :]
    y0 = rhs[:, 0, :] * piv[0:1, :]
    mine = pl.ds(pl.multiple_of(xx * 8, 8), 8)

    load_uc.wait()
    ucf[...] = uc[...].astype(F32).reshape(ucf.shape)
    for d in range(16):
        ct[d] = ucf[pl.ds(d, 128, stride=16), :].astype(BF16)
    cr[0] = ct[0]
    for d in (3, 13, 4, 12, 5, 11, 6, 10, 7, 9, 8, 1, 15, 2, 14):
        push(ct.at[d], cr.at[d], 7, at_row(d))
    load_u0.wait()
    for d in x_far:
        push(u.at[0, 1], l10g.at[d], 4, at_x(d))
    for d in x_far:
        push(inv.at[0], m0g.at[d], 5, at_x(d))
    l10g[0] = u[0, 1]
    m0g[0] = inv[0]
    s0 = below_sum(0)
    ss[...] = jnp.concatenate([s0, y0], axis=1)
    for d in x_far:
        start = pl.multiple_of(lax.rem(xx + d, XS) * 8, 8)
        push(ss.at[pl.ds(start, 8)], sg.at[d], 3, at_x(d))
    sg[0] = ss[mine, :]
    pl.semaphore_wait(ready, len(x_far))

    whole(p1r.at[pl.ds(0, 15)], 0).wait_recv()
    s1 = p1r[0].astype(F32)
    for k in range(1, ROWS):
        s1 += p1r[k].astype(F32)
    s1 = jnp.concatenate([s1[:, :64], s1[:, 64:]], axis=0)
    part = dot((y1 - s1).astype(BF16), inv[1], NN).astype(p3s.dtype)
    p3s[...] = part.reshape(4, 8, 128)
    for dx, dy in col_far:
        push(p3s.at[lax.rem(xx + dx, XS)], p3.at[col], 6, at_col(dx, dy))
    p3[col] = p3s[xx]
    whole(sg.at[pl.ds(1, 3)], 3).wait_recv()
    below0 = jnp.concatenate([sg[j][:, :64] for j in range(XS)], axis=1)
    y0 = jnp.concatenate([sg[j][:, 64:] for j in range(XS)], axis=1)
    whole(l10g.at[pl.ds(1, 3)], 4).wait_recv()
    whole(m0g.at[pl.ds(1, 3)], 5).wait_recv()

    whole(p3.at[pl.ds(0, 31)], 6).wait_recv()
    x1 = p3[0].astype(F32)
    for k in range(1, XS * YS):
        x1 += p3[k].astype(F32)
    xfull[1, mine, :] = x1
    s0 = (below0 + dot(x1.astype(BF16), l10g[...].reshape(256, 128), NT)).astype(BF16)
    p4s[pl.ds(0, 8), :] = s0[:, :128]
    p4s[pl.ds(8, 8), :] = s0[:, 128:]
    for d in row_far:
        push(p4s, p4.at[row], 8, at_row(d))
    p4[row] = p4s[...]
    for d in x_far:
        push(xfull.at[1, mine], xfull.at[1, mine], 9, at_x(d))

    load_map.wait()
    load_cnt.wait()
    load_rc.wait()
    child = col // (XS * YS // 2)
    whole(cr.at[pl.ds(1, 15)], 7).wait_recv()
    w0 = jnp.zeros((128, 128), F32)
    for d in range(16):
        slot = d * 16 + lax.rem(row - d + 16, 16)
        wanted = jnp.logical_and(slot < cnt[child], cmap[child, slot] // ROWS == 0)
        w0 += jnp.where(wanted, cr[d].astype(F32), 0.0)
    w0s[...] = w0.astype(BF16)
    w0g[0] = w0s[...]
    for d in x_far:
        push(w0s, w0g.at[d], 10, at_x(d))

    whole(xfull.at[1, pl.ds(0, 24)], 9).wait_recv()
    x1 = xfull[1]
    x_out[:, 1, :] = x1
    xb[1] = x1.astype(BF16)
    total = jnp.zeros((32, 128), F32)
    for d in range(16):
        slot = d * 16 + lax.rem(row - d + 16, 16)
        term = dot(xb[cmap[child, slot] // ROWS], cr[d], NT)
        total += jnp.where(slot < cnt[child], term, 0.0)
    p6s[...] = total.reshape(4, 8, 128)
    for d in x_far:
        push(p6s.at[lax.rem(xx + d, XS)], p6.at[d], 12, at_x(d))
    p6[0] = p6s[xx]

    whole(p4.at[pl.ds(0, 15)], 8).wait_recv()
    s0 = p4[0].astype(F32)
    for k in range(1, ROWS):
        s0 += p4[k].astype(F32)
    t0 = (y0 - jnp.concatenate([s0[:8], s0[8:]], axis=1)).astype(BF16)
    part = dot(t0, m0g[...].reshape(256, 128), NN)
    p5s[...] = part
    p5[yy] = part
    for d in y_far:
        push(p5s, p5.at[yy], 11, at_y(d))

    whole(w0g.at[pl.ds(1, 3)], 10).wait_recv()
    whole(p6.at[pl.ds(1, 3)], 12).wait_recv()

    whole(p5.at[pl.ds(0, 7)], 11).wait_recv()
    x0 = p5[0]
    for k in range(1, YS):
        x0 += p5[k]
    late = dot(x0.astype(BF16), w0g[...].reshape(512, 128), NT)
    for j in range(XS):
        p7s[j] = (p6[j] + late[:, 128 * j:128 * j + 128]).astype(BF16)
    for dr, dx in row_x_far:
        push(p7s.at[(XS - dx) % XS], p7.at[xx * ROWS + row], 14, at_row_x(dr, dx))
    p7[xx * ROWS + row] = p7s[0]
    xfull[0, mine, :] = x0
    for d in x_far:
        push(xfull.at[0, mine], xfull.at[0, mine], 15, at_x(d))

    whole(xfull.at[0, pl.ds(0, 24)], 15).wait()
    x_out[:, 0, :] = xfull[0]
    save_x = load(x_out, x_hbm, 10)

    whole(p7.at[pl.ds(0, 63)], 14).wait()
    for j in range(XS):
        late = p7[j * ROWS].astype(F32)
        for k in range(1, ROWS):
            late += p7[j * ROWS + k].astype(F32)
        c_out[pl.ds(8 * j, 8), :] = rc[pl.ds(8 * j, 8), :] - late
    save_c = load(c_out, c_hbm, 11)
    whole(p1r.at[pl.ds(0, 15)], 0).wait_send()
    whole(sg.at[pl.ds(1, 3)], 3).wait_send()
    whole(l10g.at[pl.ds(1, 3)], 4).wait_send()
    whole(m0g.at[pl.ds(1, 3)], 5).wait_send()
    whole(p3.at[pl.ds(0, 31)], 6).wait_send()
    whole(cr.at[pl.ds(1, 15)], 7).wait_send()
    whole(p4.at[pl.ds(0, 15)], 8).wait_send()
    whole(xfull.at[1, pl.ds(0, 24)], 9).wait_send()
    whole(w0g.at[pl.ds(1, 3)], 10).wait_send()
    whole(p5.at[pl.ds(0, 7)], 11).wait_send()
    whole(p6.at[pl.ds(1, 3)], 12).wait_send()

    save_x.wait()
    save_c.wait()


def local(
    u_front,
    inverse_blocks,
    rhs_window,
    pivot_inverse,
    below_solution,
    u_child,
    rhs_child,
    child_map,
    child_counts,
):
    u = jnp.transpose(u_front, (0, 2, 1, 3))
    inv = jnp.transpose(inverse_blocks, (0, 2, 1, 3)).reshape(2, 64, 128)
    below = jnp.transpose(below_solution, (1, 0, 2))
    vm = pltpu.VMEM
    return pl.pallas_call(
        kernel,
        out_shape=(
            jax.ShapeDtypeStruct((32, 2, 128), F32),
            jax.ShapeDtypeStruct((32, 128), F32),
        ),
        in_specs=[pl.BlockSpec(memory_space=pl.ANY)] * 9,
        out_specs=(pl.BlockSpec(memory_space=pl.ANY), pl.BlockSpec(memory_space=pl.ANY)),
        scratch_shapes=[
            vm((2, 25, 64, 128), BF16),
            vm((2, 64, 128), BF16),
            vm((32, 2, 64), F32),
            vm((2, 64), F32),
            vm((25, 32, 128), BF16),
            vm((128, 16, 128), BF16),
            vm((32, 128), F32),
            pltpu.SMEM((2, 256), jnp.int32),
            pltpu.SMEM((2,), jnp.int32),
            vm((2048, 128), F32),
            vm((16, 128, 128), BF16),
            vm((16, 128, 128), BF16),
            vm((2, 32, 128), F32),
            vm((4, 64, 128), BF16),
            vm((4, 64, 128), BF16),
            vm((128, 128), BF16),
            vm((4, 128, 128), BF16),
            vm((32, 128), F32),
            vm((4, 8, 128), F32),
            vm((16, 128), BF16),
            vm((16, 16, 128), BF16),
            vm((4, 8, 128), F32),
            vm((32, 8, 128), F32),
            vm((16, 128), BF16),
            vm((16, 16, 128), BF16),
            vm((8, 128), F32),
            vm((8, 8, 128), F32),
            vm((4, 8, 128), F32),
            vm((4, 8, 128), F32),
            vm((4, 8, 128), BF16),
            vm((64, 8, 128), BF16),
            vm((32, 2, 128), F32),
            vm((32, 128), F32),
            pltpu.SemaphoreType.DMA((12,)),
            pltpu.SemaphoreType.DMA((16,)),
            pltpu.SemaphoreType.DMA((16,)),
            pltpu.SemaphoreType.REGULAR,
        ],
        compiler_params=pltpu.CompilerParams(
            collective_id=0, has_side_effects=True, vmem_limit_bytes=60 << 20
        ),
        name="solve",
    )(u, inv, rhs_window, pivot_inverse, below, u_child, rhs_child, child_map, child_counts)


def solution(mesh):
    return jax.shard_map(
        local,
        mesh=mesh,
        in_specs=(
            P(None, "col", None, "row"),
            P(None, "col", None, "row"),
            P(None, None, "col"),
            P(None, "col"),
            P(None, None, "row"),
            P("col", None, "row"),
            P(None, "col"),
            P(),
            P(),
        ),
        out_specs=(P(None, None, "row"), P(None, "col")),
        check_vma=False,
    )
```

```python
import functools

import jax
import jax.numpy as jnp
from jax import lax
from jax.experimental import pallas as pl
from jax.experimental.pallas import tpu as pltpu
from jax.sharding import PartitionSpec as P

MESH = pl.DeviceIdType.MESH
F32 = jnp.float32
BF16 = jnp.bfloat16
CORES = 2
ZS = 8
XS = 4
YS = 8
ROWS = ZS * CORES
NT = (((1,), (1,)), ((), ()))
NN = (((1,), (0,)), ((), ()))


def dot(a, b, dims):
    return lax.dot_general(a, b, dims, preferred_element_type=F32)


def kernel(
    u_hbm, inv_hbm, rhs_hbm, piv_hbm, below_hbm, uc_hbm, rc_hbm, map_hbm, cnt_hbm,
    x_hbm, c_hbm,
    u, inv, rhs, piv, xb, uc, rc, cmap, cnt,
    ucf, ct, cr, xfull,
    l10g, m0g, w0s, w0g, ss, sg,
    p1s, p1r,
    p3s, p3, p4s, p4, p5s, p5,
    p6s, p6, p7s, p7,
    x_out, c_out, in_sem, send, recv, ready,
):
    row = lax.axis_index("row")
    col = lax.axis_index("col")
    z = row // CORES
    core = lax.rem(row, CORES)
    xx = col // YS
    yy = lax.rem(col, YS)

    def at_row(d):
        return (lax.rem(row + d, ROWS), col)

    def at_x(d):
        return (row, lax.rem(xx + d, XS) * YS + yy)

    def at_y(d):
        return (row, xx * YS + lax.rem(yy + d, YS))

    def at_row_x(dr, dx):
        return (lax.rem(row + dr, ROWS), lax.rem(xx + dx, XS) * YS + yy)

    def at_col(dx, dy):
        return (row, lax.rem(xx + dx, XS) * YS + lax.rem(yy + dy, YS))

    sibling = (z * CORES + (1 - core), col)
    y_far = (4, 3, 5, 2, 6, 1, 7)
    x_far = (2, 1, 3)
    row_far = (8, 9, 7, 10, 6, 11, 5, 12, 4, 13, 3, 14, 2, 15, 1)
    col_far = [(dx, dy) for dx in (2, 1, 3) for dy in (4, 3, 5, 2, 6, 1, 7, 0)] + [(0, dy) for dy in (4, 3, 5, 2, 6, 1, 7)]
    row_x_far = [(dr, dx) for dx in (2, 1, 3) for dr in row_far + (0,)] + [(dr, 0) for dr in row_far]

    def load(src, dst, index):
        copy = pltpu.make_async_copy(src, dst, in_sem.at[index])
        copy.start()
        return copy

    barrier = pltpu.get_barrier_semaphore()

    def greet(device):
        pl.semaphore_signal(barrier, inc=1, device_id=device, device_id_type=MESH)

    load_x = load(below_hbm, xb.at[pl.ds(2, 23)], 0)
    load_u1 = load(u_hbm.at[1], u.at[1], 1)
    for d in row_far:
        greet(at_row(d))
    for d in y_far:
        greet(at_y(d))
    for d in x_far:
        greet(at_x(d))
    load_rhs = load(rhs_hbm, rhs, 2)
    load_piv = load(piv_hbm, piv, 3)
    load_inv = load(inv_hbm, inv, 4)
    load_u0 = load(u_hbm.at[0], u.at[0], 5)
    load_uc = load(uc_hbm, uc, 6)
    load_rc = load(rc_hbm, rc, 7)
    load_map = load(map_hbm, cmap, 8)
    load_cnt = load(cnt_hbm, cnt, 9)

    def push(src, dst, phase, device):
        pltpu.make_async_remote_copy(
            src_ref=src, dst_ref=dst, send_sem=send.at[phase], recv_sem=recv.at[phase],
            device_id=device, device_id_type=MESH,
        ).start()

    def whole(ref, phase):
        return pltpu.make_async_remote_copy(
            src_ref=ref, dst_ref=ref, send_sem=send.at[phase], recv_sem=recv.at[phase],
            device_id=sibling, device_id_type=MESH,
        )

    xb[0] = jnp.zeros(xb.shape[1:], BF16)
    xb[1] = jnp.zeros(xb.shape[1:], BF16)

    def below_sum(panel):
        total = dot(xb[2], u[panel, 2], NT)
        for q in range(3, 25, 2):
            total += dot(
                jnp.concatenate([xb[q], xb[q + 1]], axis=1),
                jnp.concatenate([u[panel, q], u[panel, q + 1]], axis=1),
                NT,
            )
        return total

    load_x.wait()
    load_u1.wait()
    s1 = below_sum(1)
    p1s[...] = jnp.concatenate([s1[:16], s1[16:]], axis=1).astype(BF16)
    pl.semaphore_wait(barrier, len(row_far) + len(y_far) + len(x_far))
    for d in row_far:
        push(p1s, p1r.at[row], 0, at_row(d))
    p1r[row] = p1s[...]
    for d in x_far:
        pl.semaphore_signal(ready, inc=1, device_id=at_x(d), device_id_type=MESH)
    load_rhs.wait()
    load_piv.wait()
    load_inv.wait()
    y1 = rhs[:, 1, :] * piv[1:2, :]
    y0 = rhs[:, 0, :] * piv[0:1, :]
    mine = pl.ds(pl.multiple_of(xx * 8, 8), 8)

    load_uc.wait()
    ucf[...] = uc[...].astype(F32).reshape(ucf.shape)
    for d in range(16):
        ct[d] = ucf[pl.ds(d, 128, stride=16), :].astype(BF16)
    cr[0] = ct[0]
    for d in (5, 11, 6, 10, 7, 9, 8):
        push(ct.at[d], cr.at[d], 7, at_row(d))
    load_u0.wait()
    for d in x_far:
        push(u.at[0, 1], l10g.at[d], 4, at_x(d))
    for d in x_far:
        push(inv.at[0], m0g.at[d], 5, at_x(d))
    l10g[0] = u[0, 1]
    m0g[0] = inv[0]
    s0 = below_sum(0)
    ss[...] = jnp.concatenate([s0, y0], axis=1)
    for d in x_far:
        start = pl.multiple_of(lax.rem(xx + d, XS) * 8, 8)
        push(ss.at[pl.ds(start, 8)], sg.at[d], 3, at_x(d))
    sg[0] = ss[mine, :]
    pl.semaphore_wait(ready, len(x_far))

    whole(p1r.at[pl.ds(0, 15)], 0).wait_recv()
    s1 = p1r[0].astype(F32)
    for k in range(1, ROWS):
        s1 += p1r[k].astype(F32)
    s1 = jnp.concatenate([s1[:, :64], s1[:, 64:]], axis=0)
    part = dot((y1 - s1).astype(BF16), inv[1], NN).astype(p3s.dtype)
    p3s[...] = part.reshape(4, 8, 128)
    for dx, dy in col_far:
        push(p3s.at[lax.rem(xx + dx, XS)], p3.at[col], 6, at_col(dx, dy))
    p3[col] = p3s[xx]
    for d in (1, 15, 2, 14, 3, 13, 4, 12):
        push(ct.at[d], cr.at[d], 7, at_row(d))
    whole(sg.at[pl.ds(1, 3)], 3).wait_recv()
    below0 = jnp.concatenate([sg[j][:, :64] for j in range(XS)], axis=1)
    y0 = jnp.concatenate([sg[j][:, 64:] for j in range(XS)], axis=1)
    whole(l10g.at[pl.ds(1, 3)], 4).wait_recv()
    whole(m0g.at[pl.ds(1, 3)], 5).wait_recv()

    whole(p3.at[pl.ds(0, 31)], 6).wait_recv()
    x1 = p3[0].astype(F32)
    for k in range(1, XS * YS):
        x1 += p3[k].astype(F32)
    xfull[1, mine, :] = x1
    s0 = (below0 + dot(x1.astype(BF16), l10g[...].reshape(256, 128), NT)).astype(BF16)
    p4s[pl.ds(0, 8), :] = s0[:, :128]
    p4s[pl.ds(8, 8), :] = s0[:, 128:]
    for d in row_far:
        push(p4s, p4.at[row], 8, at_row(d))
    p4[row] = p4s[...]
    for d in x_far:
        push(xfull.at[1, mine], xfull.at[1, mine], 9, at_x(d))

    load_map.wait()
    load_cnt.wait()
    load_rc.wait()
    child = col // (XS * YS // 2)
    whole(cr.at[pl.ds(1, 15)], 7).wait_recv()
    w0 = jnp.zeros((128, 128), F32)
    for d in range(16):
        slot = d * 16 + lax.rem(row - d + 16, 16)
        wanted = jnp.logical_and(slot < cnt[child], cmap[child, slot] // ROWS == 0)
        w0 += jnp.where(wanted, cr[d].astype(F32), 0.0)
    w0s[...] = w0.astype(BF16)
    w0g[0] = w0s[...]
    for d in x_far:
        push(w0s, w0g.at[d], 10, at_x(d))

    whole(xfull.at[1, pl.ds(0, 24)], 9).wait_recv()
    x1 = xfull[1]
    x_out[:, 1, :] = x1
    xb[1] = x1.astype(BF16)
    total = jnp.zeros((32, 128), F32)
    for d in range(16):
        slot = d * 16 + lax.rem(row - d + 16, 16)
        term = dot(xb[cmap[child, slot] // ROWS], cr[d], NT)
        total += jnp.where(slot < cnt[child], term, 0.0)
    p6s[...] = total.reshape(4, 8, 128)
    for d in x_far:
        push(p6s.at[lax.rem(xx + d, XS)], p6.at[d], 12, at_x(d))
    p6[0] = p6s[xx]

    whole(p4.at[pl.ds(0, 15)], 8).wait_recv()
    s0 = p4[0].astype(F32)
    for k in range(1, ROWS):
        s0 += p4[k].astype(F32)
    t0 = (y0 - jnp.concatenate([s0[:8], s0[8:]], axis=1)).astype(BF16)
    part = dot(t0, m0g[...].reshape(256, 128), NN)
    p5s[...] = part
    p5[yy] = part
    for d in y_far:
        push(p5s, p5.at[yy], 11, at_y(d))

    whole(w0g.at[pl.ds(1, 3)], 10).wait_recv()
    whole(p6.at[pl.ds(1, 3)], 12).wait_recv()

    whole(p5.at[pl.ds(0, 7)], 11).wait_recv()
    x0 = p5[0]
    for k in range(1, YS):
        x0 += p5[k]
    late = dot(x0.astype(BF16), w0g[...].reshape(512, 128), NT)
    for j in range(XS):
        p7s[j] = (p6[j] + late[:, 128 * j:128 * j + 128]).astype(BF16)
    for dr, dx in row_x_far:
        push(p7s.at[(XS - dx) % XS], p7.at[xx * ROWS + row], 14, at_row_x(dr, dx))
    p7[xx * ROWS + row] = p7s[0]
    xfull[0, mine, :] = x0
    for d in x_far:
        push(xfull.at[0, mine], xfull.at[0, mine], 15, at_x(d))

    whole(xfull.at[0, pl.ds(0, 24)], 15).wait()
    x_out[:, 0, :] = xfull[0]
    save_x = load(x_out, x_hbm, 10)

    whole(p7.at[pl.ds(0, 63)], 14).wait()
    for j in range(XS):
        late = p7[j * ROWS].astype(F32)
        for k in range(1, ROWS):
            late += p7[j * ROWS + k].astype(F32)
        c_out[pl.ds(8 * j, 8), :] = rc[pl.ds(8 * j, 8), :] - late
    save_c = load(c_out, c_hbm, 11)
    whole(p1r.at[pl.ds(0, 15)], 0).wait_send()
    whole(sg.at[pl.ds(1, 3)], 3).wait_send()
    whole(l10g.at[pl.ds(1, 3)], 4).wait_send()
    whole(m0g.at[pl.ds(1, 3)], 5).wait_send()
    whole(p3.at[pl.ds(0, 31)], 6).wait_send()
    whole(cr.at[pl.ds(1, 15)], 7).wait_send()
    whole(p4.at[pl.ds(0, 15)], 8).wait_send()
    whole(xfull.at[1, pl.ds(0, 24)], 9).wait_send()
    whole(w0g.at[pl.ds(1, 3)], 10).wait_send()
    whole(p5.at[pl.ds(0, 7)], 11).wait_send()
    whole(p6.at[pl.ds(1, 3)], 12).wait_send()

    save_x.wait()
    save_c.wait()


def local(
    u_front,
    inverse_blocks,
    rhs_window,
    pivot_inverse,
    below_solution,
    u_child,
    rhs_child,
    child_map,
    child_counts,
):
    u = jnp.transpose(u_front, (0, 2, 1, 3))
    inv = jnp.transpose(inverse_blocks, (0, 2, 1, 3)).reshape(2, 64, 128)
    below = jnp.transpose(below_solution, (1, 0, 2))
    vm = pltpu.VMEM
    return pl.pallas_call(
        kernel,
        out_shape=(
            jax.ShapeDtypeStruct((32, 2, 128), F32),
            jax.ShapeDtypeStruct((32, 128), F32),
        ),
        in_specs=[pl.BlockSpec(memory_space=pl.ANY)] * 9,
        out_specs=(pl.BlockSpec(memory_space=pl.ANY), pl.BlockSpec(memory_space=pl.ANY)),
        scratch_shapes=[
            vm((2, 25, 64, 128), BF16),
            vm((2, 64, 128), BF16),
            vm((32, 2, 64), F32),
            vm((2, 64), F32),
            vm((25, 32, 128), BF16),
            vm((128, 16, 128), BF16),
            vm((32, 128), F32),
            pltpu.SMEM((2, 256), jnp.int32),
            pltpu.SMEM((2,), jnp.int32),
            vm((2048, 128), F32),
            vm((16, 128, 128), BF16),
            vm((16, 128, 128), BF16),
            vm((2, 32, 128), F32),
            vm((4, 64, 128), BF16),
            vm((4, 64, 128), BF16),
            vm((128, 128), BF16),
            vm((4, 128, 128), BF16),
            vm((32, 128), F32),
            vm((4, 8, 128), F32),
            vm((16, 128), BF16),
            vm((16, 16, 128), BF16),
            vm((4, 8, 128), F32),
            vm((32, 8, 128), F32),
            vm((16, 128), BF16),
            vm((16, 16, 128), BF16),
            vm((8, 128), F32),
            vm((8, 8, 128), F32),
            vm((4, 8, 128), F32),
            vm((4, 8, 128), F32),
            vm((4, 8, 128), BF16),
            vm((64, 8, 128), BF16),
            vm((32, 2, 128), F32),
            vm((32, 128), F32),
            pltpu.SemaphoreType.DMA((12,)),
            pltpu.SemaphoreType.DMA((16,)),
            pltpu.SemaphoreType.DMA((16,)),
            pltpu.SemaphoreType.REGULAR,
        ],
        compiler_params=pltpu.CompilerParams(
            collective_id=0, has_side_effects=True, vmem_limit_bytes=60 << 20
        ),
        name="solve",
    )(u, inv, rhs_window, pivot_inverse, below, u_child, rhs_child, child_map, child_counts)


def solution(mesh):
    return jax.shard_map(
        local,
        mesh=mesh,
        in_specs=(
            P(None, "col", None, "row"),
            P(None, "col", None, "row"),
            P(None, None, "col"),
            P(None, "col"),
            P(None, None, "row"),
            P("col", None, "row"),
            P(None, "col"),
            P(),
            P(),
        ),
        out_specs=(P(None, None, "row"), P(None, "col")),
        check_vma=False,
    )
```
